256 devices in a mesh: seq: 64 (over z, x, core), tp: 4 (over y).
Axes of the slice: x: 4, y: 4, z: 8, core: 2. Of those that a mesh axis runs over, the one named last changes fastest.
Arguments:
- queries: bfloat16 [16384, 4096], P('seq', 'tp'), may hold values from -6 to 6
- vocab_rows: bfloat16 [131072, 1024], P('seq', 'tp'), may hold values from -36 to 36
- neighbour_ids: int32 [256, 2, 128], P('seq'), may hold values from 0 to 131071, as said below
- w_in: bfloat16 [1024, 4096], P(None, 'tp'), may hold values from -0.1875 to 0.1875
- w_out: bfloat16 [4096, 1024], P('tp'), may hold values from -0.09375 to 0.09375
- w_key: bfloat16 [1024, 4096], P(None, 'tp'), may hold values from -0.1875 to 0.1875
- w_value: bfloat16 [1024, 4096], P(None, 'tp'), may hold values from -0.1875 to 0.1875
Outputs:
- cross_out: bfloat16 [16384, 4096], P('seq', 'tp')
The draws below stay inside these ranges and needn't reach their ends.
Inputs may be any that keep to these rules, and one draw needn't show every extreme that they name: `neighbour_ids`: the owner of id i is i // 2048. Among the neighbour ids of the groups of one index of seq, at most 32 have one owner; some owner has exactly 32 among those of every index.
All inputs are finite; a program needn't handle non-finite values.
Results may differ from the reference program's by a relative error of at most 0.0095.
Values may be sent and summed in bfloat16 or wider, within the bound.
A program may use at most 64 MiB of HBM per device.

```python
import math
import jax
import jax.numpy as jnp
from jax import lax

D_ENC = 1024
ENC_FF = 4096
HEADS = 32
HEAD_WIDTH = 128
VOC_DEV = 2048
GROUP = 64
NBRS = 2
NLEN = 128
TOK_DEV = 256
TOKENS = 16384
SEQLEN = 16384
VOCAB = 131072
CAP = 32


def draw_vocab_rows(key, part):
    first, second, third = jax.random.split(key, 3)
    col_scale = jnp.exp(jax.random.uniform(third, (1, D_ENC), jnp.float32, math.log(0.3), math.log(3.0)))
    base = jnp.clip(jax.random.normal(first, (VOCAB, D_ENC), jnp.float32), -4.0, 4.0)
    row_scale = jnp.exp(jax.random.uniform(second, (VOCAB, 1), jnp.float32, math.log(0.3), math.log(3.0)))
    return (base * row_scale * col_scale).astype(jnp.bfloat16)


def draw_neighbour_ids(key, part):
    owners = VOCAB // VOC_DEV
    rows = TOK_DEV // GROUP * NBRS * NLEN
    spread = max(rows - CAP, 1)
    hot_key, block_key = jax.random.split(key)
    hot = jax.random.randint(hot_key, (), 0, owners)

    def one_block(bkey):
        first, second, third = jax.random.split(bkey, 3)
        others = (hot + 1 + jax.random.permutation(first, owners - 1)) % owners
        slots = jnp.arange(rows, dtype=jnp.int32)
        pick = jnp.clip((slots - CAP) * (owners - 1) // spread, 0, owners - 2)
        owner = jnp.where(slots < CAP, hot, others[pick])
        owner = jax.random.permutation(second, owner)
        return owner * VOC_DEV + jax.random.randint(third, (rows,), 0, VOC_DEV)
    ids = jax.vmap(one_block)(jax.random.split(block_key, owners))
    return ids.reshape(TOKENS // GROUP, NBRS, NLEN).astype(jnp.int32)


def level_of(key, extent, cuts, low, high):
    loudness, own = 1.0, jax.random.fold_in(key, 6)
    for axis_at, blocks in cuts:
        draws = jnp.exp(jax.random.uniform(jax.random.fold_in(own, axis_at), (blocks,), jnp.float32, low / len(cuts), high / len(cuts)))
        loudness = loudness * jnp.repeat(draws, extent[axis_at] // blocks).reshape([-1 if axis == axis_at else 1 for axis in range(len(extent))])
    return loudness


def scatter_about(stream_key, shape, deviation, most, cuts=(), kind=jnp.bfloat16):
    values = jax.random.normal(stream_key, shape, jnp.float32) * deviation
    if len(cuts) > 0:
        values = level_of(stream_key, shape, cuts, -0.22, 0.18) * values
    return jnp.clip(values, min=-most, max=most).astype(kind)


def setup_inputs(seed: int = 0) -> dict:
    key_of = jax.random.split(jax.random.key(seed), 8)
    queries = scatter_about(key_of[0], (TOKENS, HEADS * HEAD_WIDTH), 1.0, 6.0, ((0, 64), (1, 4)))
    vocab_rows = draw_vocab_rows(jax.random.fold_in(key_of[7], 71), 0)
    neighbour_ids = draw_neighbour_ids(jax.random.fold_in(key_of[7], 71), 0)
    w_in = scatter_about(key_of[3], (D_ENC, ENC_FF), D_ENC ** -0.5, 0.1875, ((1, 4),))
    w_out = scatter_about(key_of[4], (ENC_FF, D_ENC), ENC_FF ** -0.5, 0.09375, ((0, 4),))
    w_key = scatter_about(key_of[5], (D_ENC, HEADS * HEAD_WIDTH), D_ENC ** -0.5, 0.1875, ((1, 4),))
    w_value = scatter_about(key_of[6], (D_ENC, HEADS * HEAD_WIDTH), D_ENC ** -0.5, 0.1875, ((1, 4),))
    return dict(queries=queries, vocab_rows=vocab_rows, neighbour_ids=neighbour_ids, w_in=w_in, w_out=w_out, w_key=w_key, w_value=w_value)


def encode(emb, w_in, w_out):
    values = emb.astype(jnp.float32)
    normed = (values * lax.rsqrt(lax.optimization_barrier(jnp.mean(values * values, axis=-1, keepdims=True)) + 1e-06)).astype(emb.dtype)
    inner = jax.nn.gelu(jnp.dot(normed, w_in, preferred_element_type=jnp.float32), approximate=True).astype(emb.dtype)
    return (values + jnp.dot(inner, w_out, preferred_element_type=jnp.float32)).astype(emb.dtype)

def attend(q_rows, keys, values):
    count = q_rows.shape[0]
    width = q_rows.shape[1]
    heads = width // HEAD_WIDTH
    kcount = keys.shape[0]
    decoder_query = q_rows.astype(jnp.float32).reshape(count, heads, HEAD_WIDTH)
    neighbour_key_heads = keys.astype(jnp.float32).reshape(kcount, heads, HEAD_WIDTH)
    neighbour_value_heads = values.astype(jnp.float32).reshape(kcount, heads, HEAD_WIDTH)
    attention_logits = jnp.einsum('xjy,bjy->jxb', decoder_query, neighbour_key_heads) * HEAD_WIDTH ** (-0.5)
    expo = jnp.exp(attention_logits)
    attention_probs = (expo / lax.optimization_barrier(jnp.sum(expo, axis=-1, keepdims=True))).astype(q_rows.dtype)
    attended_values = jnp.einsum('lwo,olu->wlu', attention_probs.astype(jnp.float32), neighbour_value_heads)
    return attended_values.reshape(count, width).astype(q_rows.dtype)

def reference(queries, vocab_rows, neighbour_ids, w_in, w_out, w_key, w_value):
    groups = neighbour_ids.shape[0]
    width = queries.shape[1]
    padded = jnp.concatenate([queries, jnp.zeros((GROUP, width), queries.dtype)], axis=0)

    def per_group(item):
        group_ids, index = item
        emb = jnp.take(vocab_rows, group_ids.reshape(-1), axis=0)
        encoded = encode(emb, w_in, w_out)
        keys = jnp.dot(encoded, w_key, preferred_element_type=jnp.float32).astype(queries.dtype)
        values = jnp.dot(encoded, w_value, preferred_element_type=jnp.float32).astype(queries.dtype)
        start = (index * GROUP + GROUP - 1).astype(jnp.int32)
        q_rows = lax.dynamic_slice_in_dim(padded, start, GROUP, 0)
        return attend(q_rows, keys, values)
    windows = lax.map(per_group, (neighbour_ids, jnp.arange(groups, dtype=jnp.int32)))
    flat = windows.reshape(groups * GROUP, width)
    shifted = jnp.concatenate([jnp.zeros((GROUP - 1, width), flat.dtype), flat[:groups * GROUP - GROUP + 1]], axis=0)
    position = jnp.arange(groups * GROUP, dtype=jnp.int32) % SEQLEN
    return jnp.where((position >= GROUP - 1)[:, None], shifted, jnp.zeros_like(shifted))
```

```python
import functools

import jax
import jax.numpy as jnp
from jax import lax
from jax.experimental import pallas as pl
from jax.experimental.pallas import tpu as pltpu
from jax.sharding import PartitionSpec as P

HEAD_WIDTH = 128
GROUP = 64
F32 = jnp.float32
BF16 = jnp.bfloat16
MESH = pl.DeviceIdType.MESH
NT = (((1,), (1,)), ((), ()))


def mm(a, b):
    return jnp.dot(a, b, preferred_element_type=F32)


def rows_kernel(n, plane, cap, ids_ref, vocab_ref, out_ref, want, req, sendb, recvb, acc, slots,
                isend, irecv, rsend, rrecv):
    me = lax.axis_index("seq")
    planes = n // plane
    mine = me // plane
    rows = ids_ref.shape[1]
    voc, feats = vocab_ref.shape
    block = plane * cap
    shift = voc.bit_length() - 1

    barrier = pltpu.get_barrier_semaphore()

    def greet(k, c):
        pl.semaphore_signal(barrier, inc=1, device_id={"seq": lax.rem(me + k, n)}, device_id_type=MESH)
        return c

    lax.fori_loop(1, n, greet, 0)

    ids = ids_ref[...]
    owner = ids >> shift
    local = ids & (voc - 1)
    hot = jnp.where(lax.broadcasted_iota(jnp.int32, (n, rows), 0) == owner, 1.0, 0.0).astype(F32)
    hot16 = hot.astype(BF16)
    before = jnp.where(
        lax.broadcasted_iota(jnp.int32, (rows, rows), 0) < lax.broadcasted_iota(jnp.int32, (rows, rows), 1), 1.0, 0.0
    ).astype(BF16)
    count = mm(hot16, before)
    rank = jnp.sum(hot * count, axis=0, keepdims=True).astype(jnp.int32)
    ranked = lax.broadcasted_iota(jnp.int32, (128, rows), 0) == rank
    low = jnp.where(ranked, (local & 255).astype(F32), 0.0).astype(BF16)
    high = jnp.where(ranked, (local >> 8).astype(F32), 0.0).astype(BF16)
    table = lax.dot_general(hot16, low, NT, preferred_element_type=F32) + 256.0 * lax.dot_general(
        hot16, high, NT, preferred_element_type=F32
    )
    table = table.astype(jnp.int32)
    for o in range(n):
        want[o] = table[o : o + 1]

    pl.semaphore_wait(barrier, n - 1)

    def ids_copy(peer):
        return pltpu.make_async_remote_copy(
            src_ref=want.at[peer], dst_ref=req.at[me], send_sem=isend.at[peer], recv_sem=irecv.at[me],
            device_id={"seq": peer}, device_id_type=MESH,
        )

    def ids_arrival(src):
        return pltpu.make_async_remote_copy(
            src_ref=want.at[src], dst_ref=req.at[src], send_sem=isend.at[src], recv_sem=irecv.at[src],
            device_id={"seq": src}, device_id_type=MESH,
        )

    def rows_copy(peer):
        return pltpu.make_async_remote_copy(
            src_ref=sendb.at[peer], dst_ref=recvb.at[me], send_sem=rsend.at[peer], recv_sem=rrecv.at[me],
            device_id={"seq": peer}, device_id_type=MESH,
        )

    def rows_arrival(src):
        return pltpu.make_async_remote_copy(
            src_ref=sendb.at[src], dst_ref=recvb.at[src], send_sem=rsend.at[src], recv_sem=rrecv.at[src],
            device_id={"seq": src}, device_id_type=MESH,
        )

    def step_of(i):
        half = (i + 1) // 2
        return lax.rem(planes // 2 + jnp.where(lax.rem(i, 2) == 1, -half, half) + planes, planes)

    def send_ids(i, c):
        to = lax.rem(mine + step_of(i), planes)
        for j in range(plane):
            peer = to * plane + j

            @pl.when(peer != me)
            def _():
                ids_copy(peer).start()

        return c

    lax.fori_loop(0, planes, send_ids, 0)
    req[me] = want[me]

    slot = (owner * cap + rank).astype(F32)
    slots[...] = jnp.transpose(jnp.broadcast_to(slot, (128, rows)))

    def answer(i, c):
        to = lax.rem(mine + step_of(i), planes)
        for j in range(plane):
            peer = to * plane + j

            @pl.when(peer != me)
            def _():
                ids_arrival(peer).wait_recv()

        asked = jnp.concatenate([req[to * plane + j] for j in range(plane)], axis=0).astype(F32)
        asked = jnp.transpose(jnp.concatenate([asked, jnp.zeros((128 - plane, 128), F32)], axis=0))
        cols = [jnp.broadcast_to(asked[:cap, j : j + 1], (cap, 128)) for j in range(plane)]
        col = jnp.concatenate(cols, axis=0)
        total = jnp.zeros((block, feats), F32)
        deep = min(256, voc)
        for v in range(0, voc, deep):
            picks = [
                jnp.where(
                    col == (lax.broadcasted_iota(jnp.int32, (block, 128), 1) + (v + w)).astype(F32), 1.0, 0.0
                ).astype(BF16)
                for w in range(0, deep, 128)
            ]
            total += mm(jnp.concatenate(picks, axis=1), vocab_ref[v : v + deep, :])
        found = total.astype(BF16)
        for j in range(plane):
            sendb[to * plane + j] = found[j * cap : (j + 1) * cap]
        for j in range(plane):
            peer = to * plane + j

            @pl.when(peer != me)
            def _():
                rows_copy(peer).start()

        return c

    lax.fori_loop(0, planes, answer, 0)
    recvb[me] = sendb[me]

    acc[...] = jnp.zeros_like(acc)

    def gather(i, c):
        source = lax.rem(mine - step_of(i) + planes, planes)
        for j in range(plane):
            src = source * plane + j

            @pl.when(src != me)
            def _():
                rows_arrival(src).wait_recv()

        first = (source * block).astype(F32)
        at = slots[...] - first
        picks = [
            jnp.where(at == (lax.broadcasted_iota(jnp.int32, (rows, 128), 1) + w).astype(F32), 1.0, 0.0).astype(BF16)
            for w in range(0, block, 128)
        ]
        got = jnp.concatenate([recvb[source * plane + j] for j in range(plane)], axis=0)
        acc[...] += mm(jnp.concatenate(picks, axis=1), got)
        return c

    lax.fori_loop(0, planes, gather, 0)
    out_ref[...] = acc[...].astype(BF16)

    def drain(k, c):
        peer = lax.rem(me + k, n)
        ids_copy(peer).wait_send()
        rows_copy(peer).wait_send()
        return c

    lax.fori_loop(1, n, drain, 0)


def fetch_rows(ids, vocab_rows, n, plane, cap):
    rows = ids.shape[1]
    feats = vocab_rows.shape[1]
    return pl.pallas_call(
        functools.partial(rows_kernel, n, plane, cap),
        out_shape=jax.ShapeDtypeStruct((rows, feats), BF16),
        in_specs=[pl.BlockSpec(memory_space=pltpu.VMEM)] * 2,
        out_specs=pl.BlockSpec(memory_space=pltpu.VMEM),
        scratch_shapes=[
            pltpu.VMEM((n, 1, 128), jnp.int32),
            pltpu.VMEM((n, 1, 128), jnp.int32),
            pltpu.VMEM((n, cap, feats), BF16),
            pltpu.VMEM((n, cap, feats), BF16),
            pltpu.VMEM((rows, feats), F32),
            pltpu.VMEM((rows, 128), F32),
            pltpu.SemaphoreType.DMA((n,)),
            pltpu.SemaphoreType.DMA((n,)),
            pltpu.SemaphoreType.DMA((n,)),
            pltpu.SemaphoreType.DMA((n,)),
        ],
        compiler_params=pltpu.CompilerParams(collective_id=0, has_side_effects=True),
    )(ids, vocab_rows)


def layer_kernel(n, groups, x_ref, q_ref, win_hbm, wout_hbm, wk_hbm, wv_hbm, out_ref,
                 win, wout, wk, wv, xb, eb, hop_r, hop_l, via_r, via_l, to_r, to_l, from_l, from_r, part, mine_p,
                 qnext, wins, head, wsem, xs, xr, es, er, rs, rr, qs, qr, hs, hr):
    tp = 4
    t = lax.axis_index("tp")
    s = lax.axis_index("seq")
    right, left, across = lax.rem(t + 1, tp), lax.rem(t + tp - 1, tp), lax.rem(t + 2, tp)
    ahead, back = lax.rem(s + 1, n), lax.rem(s + n - 1, n)
    keys = x_ref.shape[1]
    fs = x_ref.shape[2]
    width = q_ref.shape[1]
    half = keys // 2
    hidden = win.shape[1]
    heads = width // HEAD_WIDTH

    loads = [
        pltpu.make_async_copy(a, b, wsem.at[i])
        for i, (a, b) in enumerate([(win_hbm, win), (wout_hbm, wout), (wk_hbm, wk), (wv_hbm, wv)])
    ]
    for load in loads:
        load.start()

    barrier = pltpu.get_barrier_semaphore()
    for where in ({"tp": right}, {"tp": left}, {"seq": ahead}, {"seq": back}):
        pl.semaphore_signal(barrier, inc=1, device_id=where, device_id_type=MESH)
    pl.semaphore_wait(barrier, 4)

    def remote(src, dst, ssem, rsem, where):
        return pltpu.make_async_remote_copy(
            src_ref=src, dst_ref=dst, send_sem=ssem, recv_sem=rsem, device_id=where, device_id_type=MESH
        )

    RIGHT, LEFT = {"tp": right}, {"tp": left}

    def ring(buf, ssem, rsem, g):
        own = buf.at[g, 0]
        return dict(
            own_r=remote(own, buf.at[g, 1], ssem.at[g, 0], rsem.at[g, 0], RIGHT),
            own_l=remote(own, buf.at[g, 2], ssem.at[g, 1], rsem.at[g, 1], LEFT),
            fwd_r=remote(buf.at[g, 1, pl.ds(0, half)], buf.at[g, 3, pl.ds(0, half)], ssem.at[g, 2], rsem.at[g, 2], RIGHT),
            fwd_l=remote(buf.at[g, 2, pl.ds(half, half)], buf.at[g, 3, pl.ds(half, half)], ssem.at[g, 3], rsem.at[g, 3], LEFT),
        )

    gather_x = [ring(xb, xs, xr, g) for g in range(groups)]
    gather_e = [ring(eb, es, er, g) for g in range(groups)]
    reduce_p = [
        dict(
            hop_r=remote(hop_r.at[g], via_r.at[g], rs.at[g, 0], rr.at[g, 0], RIGHT),
            hop_l=remote(hop_l.at[g], via_l.at[g], rs.at[g, 1], rr.at[g, 1], LEFT),
            raw_r=remote(to_r.at[g, pl.ds(half, half)], from_l.at[g, pl.ds(half, half)], rs.at[g, 2], rr.at[g, 2], RIGHT),
            raw_l=remote(to_l.at[g, pl.ds(0, half)], from_r.at[g, pl.ds(0, half)], rs.at[g, 3], rr.at[g, 3], LEFT),
            sum_r=remote(to_r.at[g, pl.ds(0, half)], from_l.at[g, pl.ds(0, half)], rs.at[g, 4], rr.at[g, 4], RIGHT),
            sum_l=remote(to_l.at[g, pl.ds(half, half)], from_r.at[g, pl.ds(half, half)], rs.at[g, 5], rr.at[g, 5], LEFT),
        )
        for g in range(groups)
    ]
    q_back = remote(q_ref.at[pl.ds(0, GROUP)], qnext, qs.at[0], qr.at[0], {"seq": back})
    head_on = remote(wins.at[groups], head, hs.at[0], hr.at[0], {"seq": ahead})

    slices = [t, left, right, across]

    def feature(i):
        return pl.ds(pl.multiple_of(slices[i] * fs, fs), fs)

    def start_own(table, g):
        table[g]["own_r"].start()
        table[g]["own_l"].start()

    def forward(table, g):
        table[g]["own_r"].wait_recv()
        table[g]["fwd_r"].start()
        table[g]["own_l"].wait_recv()
        table[g]["fwd_l"].start()

    def complete(table, g):
        table[g]["fwd_r"].wait_recv()
        table[g]["fwd_l"].wait_recv()

    def feed(g):
        complete(gather_x, g)
        square = jnp.zeros((keys, 1), F32)
        for i in range(4):
            v = xb[g, i].astype(F32)
            square += jnp.sum(v * v, axis=-1, keepdims=True)
        scale = lax.rsqrt(square * (1.0 / (4 * fs)) + 1e-06)
        hid = jnp.zeros((keys, hidden), F32)
        for i in range(4):
            normed = (xb[g, i].astype(F32) * scale).astype(BF16)
            hid += mm(normed, win[feature(i), :])
        inner = jax.nn.gelu(hid, approximate=True).astype(BF16)
        pa = mm(inner, wout[:, feature(3)])
        hop_r[g] = pa[:half].astype(BF16)
        hop_l[g] = pa[half:].astype(BF16)
        reduce_p[g]["hop_r"].start()
        reduce_p[g]["hop_l"].start()
        pr = mm(inner, wout[:, feature(2)])
        to_r[g, pl.ds(half, half)] = pr[half:].astype(BF16)
        part[g, 0] = pr[:half]
        reduce_p[g]["raw_r"].start()
        pleft = mm(inner, wout[:, feature(1)])
        to_l[g, pl.ds(0, half)] = pleft[:half].astype(BF16)
        part[g, 1] = pleft[half:]
        reduce_p[g]["raw_l"].start()
        mine_p[g] = xb[g, 0].astype(F32) + mm(inner, wout[:, feature(0)])

    def merge(g):
        p = reduce_p[g]
        p["hop_r"].wait_recv()
        to_r[g, pl.ds(0, half)] = (part[g, 0] + via_r[g].astype(F32)).astype(BF16)
        p["sum_r"].start()
        p["hop_l"].wait_recv()
        to_l[g, pl.ds(half, half)] = (part[g, 1] + via_l[g].astype(F32)).astype(BF16)
        p["sum_l"].start()

    def encode(g):
        p = reduce_p[g]
        for name in ("raw_r", "raw_l", "sum_r", "sum_l"):
            p[name].wait_recv()
        eb[g, 0] = (mine_p[g] + from_l[g].astype(F32) + from_r[g].astype(F32)).astype(BF16)
        start_own(gather_e, g)

    scale = HEAD_WIDTH ** (-0.5)

    def shifted(rows_a, count):
        pick = lax.broadcasted_iota(jnp.int32, (GROUP, 2 * GROUP), 1) == (
            lax.broadcasted_iota(jnp.int32, (GROUP, 2 * GROUP), 0) + count
        )
        return mm(jnp.where(pick, 1.0, 0.0).astype(BF16), rows_a).astype(BF16)

    def attend(g):
        complete(gather_e, g)
        kk = jnp.zeros((keys, width), F32)
        for i in range(4):
            kk += mm(eb[g, i], wk[feature(i), :])
        kk = kk.astype(BF16)
        vv = jnp.zeros((keys, width), F32)
        for i in range(4):
            vv += mm(eb[g, i], wv[feature(i), :])
        vv = vv.astype(BF16)
        if g == groups - 1:
            q_back.wait_recv()
            both = jnp.concatenate([q_ref[g * GROUP : (g + 1) * GROUP, :], qnext[...]], axis=0)
        else:
            both = q_ref[g * GROUP : (g + 2) * GROUP, :]
        qg = shifted(both, GROUP - 1)
        for h in range(heads):
            at = slice(h * HEAD_WIDTH, (h + 1) * HEAD_WIDTH)
            logits = lax.dot_general(qg[:, at], kk[:, at], NT, preferred_element_type=F32) * scale
            expo = jnp.exp(logits)
            probs = (expo * (1.0 / jnp.sum(expo, axis=-1, keepdims=True))).astype(BF16)
            wins[g + 1, :, at] = mm(probs, vv[:, at]).astype(BF16)

    order = [groups - 1] + list(range(groups - 1))
    q_back.start()

    A0 = lambda k: start_own(gather_x, order[k])
    A1 = lambda k: forward(gather_x, order[k])
    F = lambda k: feed(order[k])
    M = lambda k: merge(order[k])
    E = lambda k: encode(order[k])
    G = lambda k: forward(gather_e, order[k])
    T = lambda k: attend(order[k])

    for g in range(groups):
        xb[g, 0] = x_ref[g]
    A0(0)
    A0(1)
    loads[0].wait()
    A1(0)
    A0(2)
    A1(1)
    loads[1].wait()
    F(0)
    A0(3)
    A1(2)
    M(0)
    F(1)
    A1(3)
    E(0)
    M(1)
    F(2)
    G(0)
    E(1)
    M(2)
    F(3)
    loads[2].wait()
    loads[3].wait()
    G(1)
    T(0)
    head_on.start()
    E(2)
    M(3)
    T(1)
    G(2)
    E(3)
    T(2)
    G(3)
    head_on.wait_recv()
    at_start = jnp.where(s == 0, 0.0, 1.0)
    wins[0] = jnp.where(at_start > 0.0, head[...].astype(F32), 0.0).astype(BF16)
    T(3)
    for b in range(groups):
        both = jnp.concatenate([wins[b], wins[b + 1]], axis=0)
        out_ref[b * GROUP : (b + 1) * GROUP, :] = shifted(both, 1)
    for table in (gather_x, gather_e, reduce_p):
        for g in range(groups):
            for copy in table[g].values():
                copy.wait_send()
    q_back.wait_send()
    head_on.wait_send()


def run_layer(x, queries, w_in, w_out, w_key, w_value, n):
    groups, keys, fs = x.shape
    tok, width = queries.shape
    half = keys // 2
    vm = lambda shape, dt=BF16: pltpu.VMEM(shape, dt)
    dma = pltpu.SemaphoreType.DMA
    return pl.pallas_call(
        functools.partial(layer_kernel, n, groups),
        out_shape=jax.ShapeDtypeStruct((tok, width), BF16),
        in_specs=[pl.BlockSpec(memory_space=pltpu.VMEM)] * 2 + [pl.BlockSpec(memory_space=pl.ANY)] * 4,
        out_specs=pl.BlockSpec(memory_space=pltpu.VMEM),
        scratch_shapes=[
            vm(w_in.shape), vm(w_out.shape), vm(w_key.shape), vm(w_value.shape),
            vm((groups, 4, keys, fs)), vm((groups, 4, keys, fs)),
            vm((groups, half, fs)), vm((groups, half, fs)), vm((groups, half, fs)), vm((groups, half, fs)),
            vm((groups, keys, fs)), vm((groups, keys, fs)), vm((groups, keys, fs)), vm((groups, keys, fs)),
            vm((groups, 2, half, fs), F32), vm((groups, keys, fs), F32),
            vm((GROUP, width)), vm((groups + 1, GROUP, width)), vm((GROUP, width)),
            dma((4,)), dma((groups, 4)), dma((groups, 4)), dma((groups, 4)), dma((groups, 4)),
            dma((groups, 6)), dma((groups, 6)), dma((1,)), dma((1,)), dma((1,)), dma((1,)),
        ],
        compiler_params=pltpu.CompilerParams(
            collective_id=1, has_side_effects=True, vmem_limit_bytes=48 * 1024 * 1024
        ),
    )(x, queries, w_in, w_out, w_key, w_value)


def per_device(n, queries, vocab_rows, neighbour_ids, w_in, w_out, w_key, w_value):
    groups = neighbour_ids.shape[0]
    ids = neighbour_ids.reshape(1, -1)
    rows = ids.shape[1]
    cap = 2 * rows // n
    plane = 8 if n % 8 == 0 else 2
    own = fetch_rows(ids, vocab_rows, n, plane, cap)
    x = own.reshape(groups, rows // groups, vocab_rows.shape[1])
    return run_layer(x, queries, w_in, w_out, w_key, w_value, n)


def solution(mesh):
    return jax.shard_map(
        functools.partial(per_device, mesh.shape["seq"]),
        mesh=mesh,
        in_specs=(
            P("seq", "tp"),
            P("seq", "tp"),
            P("seq", None, None),
            P(None, "tp"),
            P("tp", None),
            P(None, "tp"),
            P(None, "tp"),
        ),
        out_specs=P("seq", "tp"),
        check_vma=False,
    )
```

```python
import functools

import jax
import jax.numpy as jnp
from jax import lax
from jax.experimental import pallas as pl
from jax.experimental.pallas import tpu as pltpu
from jax.sharding import PartitionSpec as P

HEAD_WIDTH = 128
GROUP = 64
F32 = jnp.float32
BF16 = jnp.bfloat16
MESH = pl.DeviceIdType.MESH
PLANE = 8
NT = (((1,), (1,)), ((), ()))


def mm(a, b):
    return jnp.dot(a, b, preferred_element_type=F32)


def layer_kernel(n, groups, plane, cap, ids_ref, vocab_ref, q_ref, win_hbm, wout_hbm, wk_hbm, wv_hbm, out_ref,
                 want, req, sendb, recvb, acc, slots, win, wout, wk, wv, ob, relay_r, relay_l, xb, inner, eb,
                 qnext, wins, head,
                 wsem, isend, irecv, rsend, rrecv, dsend, drecv, ssend, srecv, asend, arecv, es, er, hs, hr):
    tp = 4
    t = lax.axis_index("tp")
    me = lax.axis_index("seq")
    right, left, across = lax.rem(t + 1, tp), lax.rem(t + tp - 1, tp), lax.rem(t + 2, tp)
    ahead, back = lax.rem(me + 1, n), lax.rem(me + n - 1, n)
    planes = n // plane
    mine = me // plane
    rows = ids_ref.shape[1]
    voc, feats = vocab_ref.shape
    block = plane * cap
    shift = voc.bit_length() - 1
    keys = rows // groups
    part = keys // 4
    wide = win.shape[1]
    hidden = win.shape[2]
    width = q_ref.shape[1]
    heads = width // HEAD_WIDTH

    base = (me // 8) * 8
    p = lax.rem(me, 8)
    core = lax.rem(me, 2)
    p_r, p_l, p_x = lax.rem(p + 2, 8), lax.rem(p + 6, 8), lax.rem(p + 4, 8)
    RIGHT, LEFT = {"tp": right}, {"tp": left}
    XR, XL, TWIN = {"seq": base + p_r}, {"seq": base + p_l}, {"seq": me + 1 - 2 * core}
    OTHER = 1 - core

    loads = [
        pltpu.make_async_copy(a, b, wsem.at[i])
        for i, (a, b) in enumerate([(win_hbm, win.at[0]), (wout_hbm, wout.at[0]), (wk_hbm, wk), (wv_hbm, wv)])
    ]
    for load in loads:
        load.start()

    barrier = pltpu.get_barrier_semaphore()

    def step_of(i):
        half = (i + 1) // 2
        return lax.rem(planes // 2 + jnp.where(lax.rem(i, 2) == 1, -half, half) + planes, planes)

    def greet(i, c):
        to = lax.rem(mine + step_of(i), planes)
        for j in range(plane):
            peer = to * plane + j

            @pl.when(peer != me)
            def _():
                pl.semaphore_signal(barrier, inc=1, device_id={"seq": peer}, device_id_type=MESH)

        return c

    lax.fori_loop(0, planes, greet, 0)
    for where in (RIGHT, LEFT):
        pl.semaphore_signal(barrier, inc=1, device_id=where, device_id_type=MESH)

    ids = ids_ref[...]
    owner = ids >> shift
    local = ids & (voc - 1)
    hot = jnp.where(lax.broadcasted_iota(jnp.int32, (n, rows), 0) == owner, 1.0, 0.0).astype(F32)
    hot16 = hot.astype(BF16)
    before = jnp.where(
        lax.broadcasted_iota(jnp.int32, (rows, rows), 0) < lax.broadcasted_iota(jnp.int32, (rows, rows), 1), 1.0, 0.0
    ).astype(BF16)
    count = mm(hot16, before)
    rank = jnp.sum(hot * count, axis=0, keepdims=True).astype(jnp.int32)
    ranked = lax.broadcasted_iota(jnp.int32, (128, rows), 0) == rank
    low = jnp.where(ranked, (local & 255).astype(F32), 0.0).astype(BF16)
    high = jnp.where(ranked, (local >> 8).astype(F32), 0.0).astype(BF16)
    table = lax.dot_general(hot16, low, NT, preferred_element_type=F32) + 256.0 * lax.dot_general(
        hot16, high, NT, preferred_element_type=F32
    )
    table = table.astype(jnp.int32)
    for o in range(n):
        want[o] = table[o : o + 1]

    pl.semaphore_wait(barrier, n - 1 + 2)

    def remote(src, dst, ssem, rsem, where):
        return pltpu.make_async_remote_copy(
            src_ref=src, dst_ref=dst, send_sem=ssem, recv_sem=rsem, device_id=where, device_id_type=MESH
        )

    def ids_copy(peer):
        return remote(want.at[peer], req.at[me], isend.at[peer], irecv.at[me], {"seq": peer})

    def ids_arrival(src):
        return remote(want.at[src], req.at[src], isend.at[src], irecv.at[src], {"seq": src})

    def rows_copy(peer):
        return remote(sendb.at[peer], recvb.at[me], rsend.at[peer], rrecv.at[me], {"seq": peer})

    def rows_arrival(src):
        return remote(sendb.at[src], recvb.at[src], rsend.at[src], rrecv.at[src], {"seq": src})

    def send_ids(i, c):
        to = lax.rem(mine + step_of(i), planes)
        for j in range(plane):
            peer = to * plane + j

            @pl.when(peer != me)
            def _():
                ids_copy(peer).start()

        return c

    lax.fori_loop(0, planes, send_ids, 0)

    quarter = wide // 4

    def a_part(c, k):
        return pl.ds(pl.multiple_of(c * (2 * quarter) + k * quarter, quarter), quarter)

    def a_half(c):
        return pl.ds(pl.multiple_of(c * (2 * quarter), 2 * quarter), 2 * quarter)

    lot = hidden // 8
    lot2 = lot // 2

    def b_lot(i):
        return pl.ds(pl.multiple_of(i * lot, lot), lot)

    def b_half(i, k):
        return pl.ds(pl.multiple_of(i * lot + k * lot2, lot2), lot2)

    in_r = [remote(win_hbm.at[a_part(core, k)], win.at[1, a_part(core, k)], dsend.at[k], drecv.at[k], RIGHT) for k in (0, 1)]
    in_l = [remote(win_hbm.at[a_part(core, k)], win.at[2, a_part(core, k)], dsend.at[2 + k], drecv.at[2 + k], LEFT) for k in (0, 1)]
    eighth = quarter // 2

    def a_sub(c, k, j):
        return pl.ds(pl.multiple_of(c * (2 * quarter) + k * quarter + j * eighth, eighth), eighth)

    def a_on(k, j):
        at = a_sub(core, k, j)
        return remote(win.at[1 + k, at], win.at[3, at], dsend.at[4 + 2 * j + k], drecv.at[4 + 2 * j + k], (RIGHT, LEFT)[k])

    def a_twin(c, k, j):
        at = a_sub(c, k, j)
        return remote(win.at[3, at], win.at[3, at], dsend.at[8 + 2 * j + k], drecv.at[8 + 2 * j + k], TWIN)

    def a_twins(c):
        both = win.at[pl.ds(1, 2), a_half(c)]
        return remote(both, both, dsend.at[12], drecv.at[12], TWIN)

    on = [[a_on(k, j) for k in (0, 1)] for j in (0, 1)]
    twin_3 = [[a_twin(core, k, j) for k in (0, 1)] for j in (0, 1)]
    twin_12 = a_twins(core)
    lot_r = remote(wout_hbm.at[b_lot(p)], wout.at[1, b_lot(p)], ssend.at[0], srecv.at[0], RIGHT)
    lot_l = remote(wout_hbm.at[b_lot(p)], wout.at[2, b_lot(p)], ssend.at[1], srecv.at[1], LEFT)
    lot_on_r = remote(wout.at[1, b_half(p, 0)], wout.at[3, b_half(p, 0)], ssend.at[2], srecv.at[2], RIGHT)
    lot_on_l = remote(wout.at[2, b_half(p, 1)], wout.at[3, b_half(p, 1)], ssend.at[3], srecv.at[3], LEFT)
    slots_of = (pl.ds(1, 2), pl.ds(3, 1))

    def share(m, at, i, where):
        both = wout.at[slots_of[m], at]
        return remote(both, both, ssend.at[4 + 8 * m + i], srecv.at[4 + 8 * m + i], where)

    x_r = [share(m, b_lot(p), 0, XR) for m in (0, 1)]
    x_l = [share(m, b_lot(p), 1, XL) for m in (0, 1)]
    x_on_r = [share(m, b_half(p_l, 0), 2, XR) for m in (0, 1)]
    x_on_l = [share(m, b_half(p_r, 1), 3, XL) for m in (0, 1)]
    twins = [[share(m, b_lot(q), 4 + i, TWIN) for i, q in enumerate((p, p_l, p_r, p_x))] for m in (0, 1)]

    def x_start(m):
        x_r[m].start()
        x_l[m].start()
        twins[m][0].start()

    def x_forward(m):
        x_r[m].wait_recv()
        x_l[m].wait_recv()
        x_on_r[m].start()
        x_on_l[m].start()
        twins[m][1].start()
        twins[m][2].start()

    def x_finish(m):
        x_on_r[m].wait_recv()
        x_on_l[m].wait_recv()
        twins[m][3].start()

    lot_r.start()
    lot_l.start()
    in_r[0].start()
    in_l[1].start()
    q_back = remote(q_ref.at[pl.ds(0, GROUP)], qnext, hs.at[0], hr.at[0], {"seq": back})
    q_back.start()
    req[me] = want[me]

    slot = (owner * cap + rank).astype(F32)
    slots[...] = jnp.transpose(jnp.broadcast_to(slot, (128, rows)))

    def answer(i, c):
        to = lax.rem(mine + step_of(i), planes)
        for j in range(plane):
            peer = to * plane + j

            @pl.when(peer != me)
            def _():
                ids_arrival(peer).wait_recv()

        @pl.when(i == 2)
        def _():
            lot_r.wait_recv()
            lot_on_r.start()
            lot_l.wait_recv()
            lot_on_l.start()
            x_start(0)
            in_r[1].start()
            in_l[0].start()

        asked = jnp.concatenate([req[to * plane + j] for j in range(plane)], axis=0).astype(F32)
        asked = jnp.transpose(jnp.concatenate([asked, jnp.zeros((128 - plane, 128), F32)], axis=0))
        cols = [jnp.broadcast_to(asked[:cap, j : j + 1], (cap, 128)) for j in range(plane)]
        col = jnp.concatenate(cols, axis=0)
        total = jnp.zeros((block, feats), F32)
        deep = min(256, voc)
        for v in range(0, voc, deep):
            picks = [
                jnp.where(
                    col == (lax.broadcasted_iota(jnp.int32, (block, 128), 1) + (v + w)).astype(F32), 1.0, 0.0
                ).astype(BF16)
                for w in range(0, deep, 128)
            ]
            total += mm(jnp.concatenate(picks, axis=1), vocab_ref[v : v + deep, :])
        found = total.astype(BF16)
        for j in range(plane):
            sendb[to * plane + j] = found[j * cap : (j + 1) * cap]
        for j in range(plane):
            peer = to * plane + j

            @pl.when(peer != me)
            def _():
                rows_copy(peer).start()

        return c

    lax.fori_loop(0, planes, answer, 0)
    recvb[me] = sendb[me]

    acc[...] = jnp.zeros_like(acc)

    def gather(i, c):
        @pl.when(i == 1)
        def _():
            in_r[0].wait_recv()
            on[0][0].start()
            on[1][0].start()
            in_l[1].wait_recv()
            on[0][1].start()
            on[1][1].start()

        @pl.when(i == 2)
        def _():
            lot_on_r.wait_recv()
            lot_on_l.wait_recv()
            x_start(1)

        @pl.when(i == 3)
        def _():
            x_forward(0)

        @pl.when(i == 5)
        def _():
            x_finish(0)
            x_forward(1)

        @pl.when(i == 6)
        def _():
            in_r[1].wait_recv()
            in_l[0].wait_recv()
            twin_12.start()

        @pl.when(i == 7)
        def _():
            x_finish(1)

        source = lax.rem(mine - step_of(i) + planes, planes)
        for j in range(plane):
            src = source * plane + j

            @pl.when(src != me)
            def _():
                rows_arrival(src).wait_recv()

        first = (source * block).astype(F32)
        at = slots[...] - first
        picks = [
            jnp.where(at == (lax.broadcasted_iota(jnp.int32, (rows, 128), 1) + w).astype(F32), 1.0, 0.0).astype(BF16)
            for w in range(0, block, 128)
        ]
        got = jnp.concatenate([recvb[source * plane + j] for j in range(plane)], axis=0)
        acc[...] += mm(jnp.concatenate(picks, axis=1), got)
        return c

    lax.fori_loop(0, planes, gather, 0)

    ob[...] = acc[...].reshape(groups, 4, part, feats).astype(BF16)
    low_part, high_part = pl.ds(0, part // 2), pl.ds(part // 2, part // 2)
    hop_r = remote(ob.at[:, across, low_part], relay_r, asend.at[0], arecv.at[0], RIGHT)
    hop_l = remote(ob.at[:, across, high_part], relay_l, asend.at[1], arecv.at[1], LEFT)
    give_r = remote(ob.at[:, right], xb.at[1], asend.at[2], arecv.at[2], RIGHT)
    give_l = remote(ob.at[:, left], xb.at[2], asend.at[3], arecv.at[3], LEFT)
    far_r = remote(relay_r, xb.at[3, :, low_part], asend.at[4], arecv.at[4], RIGHT)
    far_l = remote(relay_l, xb.at[3, :, high_part], asend.at[5], arecv.at[5], LEFT)
    hop_r.start()
    hop_l.start()
    give_r.start()
    give_l.start()
    xb[0] = ob[:, t]
    hop_r.wait_recv()
    far_r.start()
    hop_l.wait_recv()
    far_l.start()
    for j in (0, 1):
        for k in (0, 1):
            on[j][k].wait_recv()
            twin_3[j][k].start()
    for copy in (give_r, give_l, far_r, far_l):
        copy.wait_recv()

    slices = [t, left, right, across]

    def feature(i):
        return pl.ds(pl.multiple_of(slices[i] * feats, feats), feats)

    square = jnp.zeros((keys, 1), F32)
    for i in range(4):
        v = xb[i].reshape(keys, feats).astype(F32)
        square += jnp.sum(v * v, axis=-1, keepdims=True)
    scale = lax.rsqrt(square * (1.0 / wide) + 1e-06)
    normed = [(xb[i].reshape(keys, feats).astype(F32) * scale).astype(BF16) for i in range(4)]

    def twin_arrival(i):
        if i == 1:
            a_twins(OTHER).wait_recv()
        if i == 3:
            for j in (0, 1):
                for k in (0, 1):
                    a_twin(OTHER, k, j).wait_recv()

    loads[0].wait()
    for i in range(4):
        twin_arrival(i)
        hid = jnp.zeros((keys, hidden), F32)
        for f in range(4):
            hid += mm(normed[f], win[i, feature(f), :])
        inner[i] = jax.nn.gelu(hid, approximate=True).astype(BF16)
    loads[1].wait()
    for i, q in enumerate((p, p_l, p_r, p_x)):
        for m in (0, 1):
            share(m, b_lot(q + 1 - 2 * core), 4 + i, TWIN).wait_recv()
    for f in range(4):
        total = xb[f].reshape(keys, feats).astype(F32)
        for i in range(4):
            total += mm(inner[i], wout[i, :, feature(f)])
        total = total.astype(BF16)
        for g in range(groups):
            eb[g, 0, :, feature(f)] = total[g * part : (g + 1) * part]

    def ring(g):
        own = eb.at[g, 0]
        return dict(
            own_r=remote(own, eb.at[g, 1], es.at[g, 0], er.at[g, 0], RIGHT),
            own_l=remote(own, eb.at[g, 2], es.at[g, 1], er.at[g, 1], LEFT),
            fwd_r=remote(eb.at[g, 1, low_part], eb.at[g, 3, low_part], es.at[g, 2], er.at[g, 2], RIGHT),
            fwd_l=remote(eb.at[g, 2, high_part], eb.at[g, 3, high_part], es.at[g, 3], er.at[g, 3], LEFT),
        )

    table_e = [ring(g) for g in range(groups)]
    head_on = remote(wins.at[groups], head, hs.at[1], hr.at[1], {"seq": ahead})
    soft = HEAD_WIDTH ** (-0.5)

    def shifted(rows_a, by):
        pick = lax.broadcasted_iota(jnp.int32, (GROUP, 2 * GROUP), 1) == (
            lax.broadcasted_iota(jnp.int32, (GROUP, 2 * GROUP), 0) + by
        )
        return mm(jnp.where(pick, 1.0, 0.0).astype(BF16), rows_a).astype(BF16)

    def attend(g):
        table_e[g]["fwd_r"].wait_recv()
        table_e[g]["fwd_l"].wait_recv()
        enc = eb[g].reshape(keys, wide)
        kk = mm(enc, wk[...]).astype(BF16)
        vv = mm(enc, wv[...]).astype(BF16)
        if g == groups - 1:
            q_back.wait_recv()
            both = jnp.concatenate([q_ref[g * GROUP : (g + 1) * GROUP, :], qnext[...]], axis=0)
        else:
            both = q_ref[g * GROUP : (g + 2) * GROUP, :]
        qg = shifted(both, GROUP - 1)
        for h in range(heads):
            at = slice(h * HEAD_WIDTH, (h + 1) * HEAD_WIDTH)
            logits = lax.dot_general(qg[:, at], kk[:, at], NT, preferred_element_type=F32) * soft
            expo = jnp.exp(logits)
            probs = (expo * (1.0 / jnp.sum(expo, axis=-1, keepdims=True))).astype(BF16)
            wins[g + 1, :, at] = mm(probs, vv[:, at]).astype(BF16)

    order = [groups - 1] + list(range(groups - 1))

    def own_out(k):
        table_e[order[k]]["own_r"].start()
        table_e[order[k]]["own_l"].start()

    def onward(k):
        c = table_e[order[k]]
        c["own_r"].wait_recv()
        c["fwd_r"].start()
        c["own_l"].wait_recv()
        c["fwd_l"].start()

    own_out(0)
    own_out(1)
    loads[2].wait()
    loads[3].wait()
    onward(0)
    own_out(2)
    onward(1)
    own_out(3)
    attend(order[0])
    head_on.start()
    onward(2)
    attend(order[1])
    onward(3)
    attend(order[2])
    head_on.wait_recv()
    at_start = jnp.where(me == 0, 0.0, 1.0)
    wins[0] = jnp.where(at_start > 0.0, head[...].astype(F32), 0.0).astype(BF16)
    attend(order[3])
    for b in range(groups):
        both = jnp.concatenate([wins[b], wins[b + 1]], axis=0)
        out_ref[b * GROUP : (b + 1) * GROUP, :] = shifted(both, 1)

    def drain(k, c):
        peer = lax.rem(me + k, n)
        ids_copy(peer).wait_send()
        rows_copy(peer).wait_send()
        return c

    lax.fori_loop(1, n, drain, 0)
    for g in range(groups):
        for copy in table_e[g].values():
            copy.wait_send()
    for copy in in_r + in_l + on[0] + on[1] + twin_3[0] + twin_3[1] + twins[0] + twins[1] + x_r + x_l + x_on_r + x_on_l + [
        twin_12, lot_r, lot_l, lot_on_r, lot_on_l,
        hop_r, hop_l, give_r, give_l, far_r, far_l, q_back, head_on,
    ]:
        copy.wait_send()


def per_device(n, queries, vocab_rows, neighbour_ids, w_in, w_out, w_key, w_value):
    groups = neighbour_ids.shape[0]
    ids = neighbour_ids.reshape(1, -1)
    rows = ids.shape[1]
    cap = 2 * rows // n
    plane = PLANE
    feats = vocab_rows.shape[1]
    tok, width = queries.shape
    wide, hidden = w_in.shape
    keys = rows // groups
    part = keys // 4
    vm = lambda shape, dt=BF16: pltpu.VMEM(shape, dt)
    dma = pltpu.SemaphoreType.DMA
    return pl.pallas_call(
        functools.partial(layer_kernel, n, groups, plane, cap),
        out_shape=jax.ShapeDtypeStruct((tok, width), BF16),
        in_specs=[pl.BlockSpec(memory_space=pltpu.VMEM)] * 3 + [pl.BlockSpec(memory_space=pltpu.MemorySpace.HBM)] * 4,
        out_specs=pl.BlockSpec(memory_space=pltpu.VMEM),
        scratch_shapes=[
            vm((n, 1, 128), jnp.int32), vm((n, 1, 128), jnp.int32),
            vm((n, cap, feats)), vm((n, cap, feats)), vm((rows, feats), F32), vm((rows, 128), F32),
            vm((4, wide, hidden)), vm((4, hidden, wide)), vm(w_key.shape), vm(w_value.shape),
            vm((groups, 4, part, feats)),
            vm((groups, part // 2, feats)), vm((groups, part // 2, feats)),
            vm((4, groups, part, feats)), vm((4, keys, hidden)), vm((groups, 4, part, wide)),
            vm((GROUP, width)), vm((groups + 1, GROUP, width)), vm((GROUP, width)),
            dma((4,)), dma((n,)), dma((n,)), dma((n,)), dma((n,)),
            dma((13,)), dma((13,)), dma((20,)), dma((20,)), dma((6,)), dma((6,)),
            dma((groups, 4)), dma((groups, 4)), dma((2,)), dma((2,)),
        ],
        compiler_params=pltpu.CompilerParams(
            collective_id=0, has_side_effects=True, vmem_limit_bytes=58 * 1024 * 1024
        ),
    )(ids, vocab_rows, queries, w_in, w_out, w_key, w_value)


def solution(mesh):
    return jax.shard_map(
        functools.partial(per_device, mesh.shape["seq"]),
        mesh=mesh,
        in_specs=(
            P("seq", "tp"),
            P("seq", "tp"),
            P("seq", None, None),
            P(None, "tp"),
            P("tp", None),
            P(None, "tp"),
            P(None, "tp"),
        ),
        out_specs=P("seq", "tp"),
        check_vma=False,
    )
```

```python
import functools

import jax
import jax.numpy as jnp
from jax import lax
from jax.experimental import pallas as pl
from jax.experimental.pallas import tpu as pltpu
from jax.sharding import PartitionSpec as P

HEAD_WIDTH = 128
GROUP = 64
F32 = jnp.float32
BF16 = jnp.bfloat16
MESH = pl.DeviceIdType.MESH
PLANE = 8
NT = (((1,), (1,)), ((), ()))


def mm(a, b):
    return jnp.dot(a, b, preferred_element_type=F32)


def layer_kernel(n, groups, plane, cap, ids_ref, vocab_ref, q_ref, win_hbm, wout_hbm, wk_hbm, wv_hbm, wins,
                 want, req, sendb, recvb, acc, slots, win, wout, wk, wv, ob, relay_r, relay_l, xb, inner, eb,
                 qnext, head,
                 wsem, isend, irecv, rsend, rrecv, dsend, drecv, ssend, srecv, asend, arecv, es, er, hs, hr):
    tp = 4
    t = lax.axis_index("tp")
    me = lax.axis_index("seq")
    right, left, across = lax.rem(t + 1, tp), lax.rem(t + tp - 1, tp), lax.rem(t + 2, tp)
    ahead, back = lax.rem(me + 1, n), lax.rem(me + n - 1, n)
    planes = n // plane
    mine = me // plane
    rows = ids_ref.shape[1]
    voc, feats = vocab_ref.shape
    block = plane * cap
    shift = voc.bit_length() - 1
    keys = rows // groups
    part = keys // 4
    wide = win.shape[1]
    hidden = win.shape[2]
    width = q_ref.shape[1]
    heads = width // HEAD_WIDTH

    base = (me // 8) * 8
    p = lax.rem(me, 8)
    core = lax.rem(me, 2)
    p_r, p_l, p_x = lax.rem(p + 2, 8), lax.rem(p + 6, 8), lax.rem(p + 4, 8)
    RIGHT, LEFT = {"tp": right}, {"tp": left}
    XR, XL, TWIN = {"seq": base + p_r}, {"seq": base + p_l}, {"seq": me + 1 - 2 * core}
    OTHER = 1 - core

    loads = [
        pltpu.make_async_copy(a, b, wsem.at[i])
        for i, (a, b) in enumerate([(win_hbm, win.at[0]), (wout_hbm, wout.at[0]), (wk_hbm, wk), (wv_hbm, wv)])
    ]
    for load in loads:
        load.start()

    barrier = pltpu.get_barrier_semaphore()

    def step_of(i):
        half = (i + 1) // 2
        return lax.rem(planes // 2 + jnp.where(lax.rem(i, 2) == 1, -half, half) + planes, planes)

    def greet(i, c):
        to = lax.rem(mine + step_of(i), planes)
        for j in range(plane):
            peer = to * plane + j

            @pl.when(peer != me)
            def _():
                pl.semaphore_signal(barrier, inc=1, device_id={"seq": peer}, device_id_type=MESH)

        return c

    lax.fori_loop(0, planes, greet, 0)
    for where in (RIGHT, LEFT):
        pl.semaphore_signal(barrier, inc=1, device_id=where, device_id_type=MESH)

    ids = ids_ref[...]
    owner = ids >> shift
    local = ids & (voc - 1)
    hot = jnp.where(lax.broadcasted_iota(jnp.int32, (n, rows), 0) == owner, 1.0, 0.0).astype(F32)
    hot16 = hot.astype(BF16)
    before = jnp.where(
        lax.broadcasted_iota(jnp.int32, (rows, rows), 0) < lax.broadcasted_iota(jnp.int32, (rows, rows), 1), 1.0, 0.0
    ).astype(BF16)
    count = mm(hot16, before)
    rank = jnp.sum(hot * count, axis=0, keepdims=True).astype(jnp.int32)
    ranked = lax.broadcasted_iota(jnp.int32, (128, rows), 0) == rank
    low = jnp.where(ranked, (local & 255).astype(F32), 0.0).astype(BF16)
    high = jnp.where(ranked, (local >> 8).astype(F32), 0.0).astype(BF16)
    table = lax.dot_general(hot16, low, NT, preferred_element_type=F32) + 256.0 * lax.dot_general(
        hot16, high, NT, preferred_element_type=F32
    )
    table = table.astype(jnp.int32)
    for o in range(n):
        want[o] = table[o : o + 1]

    pl.semaphore_wait(barrier, n - 1 + 2)

    def remote(src, dst, ssem, rsem, where):
        return pltpu.make_async_remote_copy(
            src_ref=src, dst_ref=dst, send_sem=ssem, recv_sem=rsem, device_id=where, device_id_type=MESH
        )

    def ids_copy(peer):
        return remote(want.at[peer], req.at[me], isend.at[peer], irecv.at[me], {"seq": peer})

    def ids_arrival(src):
        return remote(want.at[src], req.at[src], isend.at[src], irecv.at[src], {"seq": src})

    def rows_copy(peer):
        return remote(sendb.at[peer], recvb.at[me], rsend.at[peer], rrecv.at[me], {"seq": peer})

    def rows_arrival(src):
        return remote(sendb.at[src], recvb.at[src], rsend.at[src], rrecv.at[src], {"seq": src})

    def send_ids(i, c):
        to = lax.rem(mine + step_of(i), planes)
        for j in range(plane):
            peer = to * plane + j

            @pl.when(peer != me)
            def _():
                ids_copy(peer).start()

        return c

    lax.fori_loop(0, planes, send_ids, 0)

    quarter = wide // 4

    def a_part(c, k):
        return pl.ds(pl.multiple_of(c * (2 * quarter) + k * quarter, quarter), quarter)

    def a_half(c):
        return pl.ds(pl.multiple_of(c * (2 * quarter), 2 * quarter), 2 * quarter)

    lot = hidden // 8
    lot2 = lot // 2

    def b_lot(i):
        return pl.ds(pl.multiple_of(i * lot, lot), lot)

    def b_half(i, k):
        return pl.ds(pl.multiple_of(i * lot + k * lot2, lot2), lot2)

    in_r = [remote(win_hbm.at[a_part(core, k)], win.at[1, a_part(core, k)], dsend.at[k], drecv.at[k], RIGHT) for k in (0, 1)]
    in_l = [remote(win_hbm.at[a_part(core, k)], win.at[2, a_part(core, k)], dsend.at[2 + k], drecv.at[2 + k], LEFT) for k in (0, 1)]
    eighth = quarter // 2

    def a_sub(c, k, j):
        return pl.ds(pl.multiple_of(c * (2 * quarter) + k * quarter + j * eighth, eighth), eighth)

    def a_on(k, j):
        at = a_sub(core, k, j)
        return remote(win.at[1 + k, at], win.at[3, at], dsend.at[4 + 2 * j + k], drecv.at[4 + 2 * j + k], (RIGHT, LEFT)[k])

    def a_twin(c, k, j):
        at = a_sub(c, k, j)
        return remote(win.at[3, at], win.at[3, at], dsend.at[8 + 2 * j + k], drecv.at[8 + 2 * j + k], TWIN)

    def a_twins(c):
        both = win.at[pl.ds(1, 2), a_half(c)]
        return remote(both, both, dsend.at[12], drecv.at[12], TWIN)

    on = [[a_on(k, j) for k in (0, 1)] for j in (0, 1)]
    twin_3 = [[a_twin(core, k, j) for k in (0, 1)] for j in (0, 1)]
    twin_12 = a_twins(core)
    lot_r = remote(wout_hbm.at[b_lot(p)], wout.at[1, b_lot(p)], ssend.at[0], srecv.at[0], RIGHT)
    lot_l = remote(wout_hbm.at[b_lot(p)], wout.at[2, b_lot(p)], ssend.at[1], srecv.at[1], LEFT)
    lot_on_r = remote(wout.at[1, b_half(p, 0)], wout.at[3, b_half(p, 0)], ssend.at[2], srecv.at[2], RIGHT)
    lot_on_l = remote(wout.at[2, b_half(p, 1)], wout.at[3, b_half(p, 1)], ssend.at[3], srecv.at[3], LEFT)
    slots_of = (pl.ds(1, 2), pl.ds(3, 1))

    def share(m, at, i, where):
        both = wout.at[slots_of[m], at]
        return remote(both, both, ssend.at[4 + 8 * m + i], srecv.at[4 + 8 * m + i], where)

    x_r = [share(m, b_lot(p), 0, XR) for m in (0, 1)]
    x_l = [share(m, b_lot(p), 1, XL) for m in (0, 1)]
    x_on_r = [share(m, b_half(p_l, 0), 2, XR) for m in (0, 1)]
    x_on_l = [share(m, b_half(p_r, 1), 3, XL) for m in (0, 1)]
    twins = [[share(m, b_lot(q), 4 + i, TWIN) for i, q in enumerate((p, p_l, p_r, p_x))] for m in (0, 1)]

    def x_start(m):
        x_r[m].start()
        x_l[m].start()
        twins[m][0].start()

    def x_forward(m):
        x_r[m].wait_recv()
        x_l[m].wait_recv()
        x_on_r[m].start()
        x_on_l[m].start()
        twins[m][1].start()
        twins[m][2].start()

    def x_finish(m):
        x_on_r[m].wait_recv()
        x_on_l[m].wait_recv()
        twins[m][3].start()

    lot_r.start()
    lot_l.start()
    in_r[0].start()
    in_l[1].start()
    q_back = remote(q_ref.at[pl.ds(0, GROUP)], qnext, hs.at[0], hr.at[0], {"seq": back})
    q_back.start()
    req[me] = want[me]

    slot = (owner * cap + rank).astype(F32)
    slots[...] = jnp.transpose(jnp.broadcast_to(slot, (128, rows)))

    def answer(i, c):
        to = lax.rem(mine + step_of(i), planes)
        for j in range(plane):
            peer = to * plane + j

            @pl.when(peer != me)
            def _():
                ids_arrival(peer).wait_recv()

        @pl.when(i == 2)
        def _():
            lot_r.wait_recv()
            lot_on_r.start()
            lot_l.wait_recv()
            lot_on_l.start()
            x_start(0)
            in_r[1].start()
            in_l[0].start()

        asked = jnp.concatenate([req[to * plane + j] for j in range(plane)], axis=0).astype(F32)
        asked = jnp.transpose(jnp.concatenate([asked, jnp.zeros((128 - plane, 128), F32)], axis=0))
        cols = [jnp.broadcast_to(asked[:cap, j : j + 1], (cap, 128)) for j in range(plane)]
        col = jnp.concatenate(cols, axis=0)
        total = jnp.zeros((block, feats), F32)
        deep = min(256, voc)
        for v in range(0, voc, deep):
            picks = [
                jnp.where(
                    col == (lax.broadcasted_iota(jnp.int32, (block, 128), 1) + (v + w)).astype(F32), 1.0, 0.0
                ).astype(BF16)
                for w in range(0, deep, 128)
            ]
            total += mm(jnp.concatenate(picks, axis=1), vocab_ref[v : v + deep, :])
        found = total.astype(BF16)
        for j in range(plane):
            sendb[to * plane + j] = found[j * cap : (j + 1) * cap]
        for j in range(plane):
            peer = to * plane + j

            @pl.when(peer != me)
            def _():
                rows_copy(peer).start()

        return c

    lax.fori_loop(0, planes, answer, 0)
    recvb[me] = sendb[me]

    acc[...] = jnp.zeros_like(acc)

    def gather(i, c):
        @pl.when(i == 1)
        def _():
            in_r[0].wait_recv()
            on[0][0].start()
            on[1][0].start()
            in_l[1].wait_recv()
            on[0][1].start()
            on[1][1].start()

        @pl.when(i == 2)
        def _():
            lot_on_r.wait_recv()
            lot_on_l.wait_recv()
            x_start(1)

        @pl.when(i == 5)
        def _():
            x_forward(0)

        @pl.when(i == 6)
        def _():
            in_r[1].wait_recv()
            in_l[0].wait_recv()
            twin_12.start()

        source = lax.rem(mine - step_of(i) + planes, planes)
        for j in range(plane):
            src = source * plane + j

            @pl.when(src != me)
            def _():
                rows_arrival(src).wait_recv()

        first = (source * block).astype(F32)
        at = slots[...] - first
        picks = [
            jnp.where(at == (lax.broadcasted_iota(jnp.int32, (rows, 128), 1) + w).astype(F32), 1.0, 0.0).astype(BF16)
            for w in range(0, block, 128)
        ]
        got = jnp.concatenate([recvb[source * plane + j] for j in range(plane)], axis=0)
        acc[...] += mm(jnp.concatenate(picks, axis=1), got)
        return c

    lax.fori_loop(0, planes, gather, 0)

    ob[...] = acc[...].reshape(groups, 4, part, feats).astype(BF16)
    low_part, high_part = pl.ds(0, part // 2), pl.ds(part // 2, part // 2)
    hop_r = remote(ob.at[:, across, low_part], relay_r, asend.at[0], arecv.at[0], RIGHT)
    hop_l = remote(ob.at[:, across, high_part], relay_l, asend.at[1], arecv.at[1], LEFT)
    give_r = remote(ob.at[:, right], xb.at[1], asend.at[2], arecv.at[2], RIGHT)
    give_l = remote(ob.at[:, left], xb.at[2], asend.at[3], arecv.at[3], LEFT)
    far_r = remote(relay_r, xb.at[3, :, low_part], asend.at[4], arecv.at[4], RIGHT)
    far_l = remote(relay_l, xb.at[3, :, high_part], asend.at[5], arecv.at[5], LEFT)
    hop_r.start()
    hop_l.start()
    give_r.start()
    give_l.start()
    xb[0] = ob[:, t]
    x_forward(1)
    hop_r.wait_recv()
    far_r.start()
    hop_l.wait_recv()
    far_l.start()
    for j in (0, 1):
        for k in (0, 1):
            on[j][k].wait_recv()
            twin_3[j][k].start()
    x_finish(0)
    for copy in (give_r, give_l, far_r, far_l):
        copy.wait_recv()

    slices = [t, left, right, across]

    def feature(i):
        return pl.ds(pl.multiple_of(slices[i] * feats, feats), feats)

    square = jnp.zeros((keys, 1), F32)
    for i in range(4):
        v = xb[i].reshape(keys, feats).astype(F32)
        square += jnp.sum(v * v, axis=-1, keepdims=True)
    scale = lax.rsqrt(square * (1.0 / wide) + 1e-06)
    normed = [(xb[i].reshape(keys, feats).astype(F32) * scale).astype(BF16) for i in range(4)]

    def twin_arrival(i):
        if i == 1:
            a_twins(OTHER).wait_recv()
        if i == 3:
            for j in (0, 1):
                for k in (0, 1):
                    a_twin(OTHER, k, j).wait_recv()

    loads[0].wait()
    for i in range(4):
        if i == 2:
            x_finish(1)
        twin_arrival(i)
        hid = jnp.zeros((keys, hidden), F32)
        for f in range(4):
            hid += mm(normed[f], win[i, feature(f), :])
        inner[i] = jax.nn.gelu(hid, approximate=True).astype(BF16)
    loads[1].wait()
    for i, q in enumerate((p, p_l, p_r, p_x)):
        for m in (0, 1):
            share(m, b_lot(q + 1 - 2 * core), 4 + i, TWIN).wait_recv()
    for f in range(4):
        total = xb[f].reshape(keys, feats).astype(F32)
        for i in range(4):
            total += mm(inner[i], wout[i, :, feature(f)])
        total = total.astype(BF16)
        for g in range(groups):
            eb[g, 0, :, feature(f)] = total[g * part : (g + 1) * part]

    def ring(g):
        own = eb.at[g, 0]
        return dict(
            own_r=remote(own, eb.at[g, 1], es.at[g, 0], er.at[g, 0], RIGHT),
            own_l=remote(own, eb.at[g, 2], es.at[g, 1], er.at[g, 1], LEFT),
            fwd_r=remote(eb.at[g, 1, low_part], eb.at[g, 3, low_part], es.at[g, 2], er.at[g, 2], RIGHT),
            fwd_l=remote(eb.at[g, 2, high_part], eb.at[g, 3, high_part], es.at[g, 3], er.at[g, 3], LEFT),
        )

    table_e = [ring(g) for g in range(groups)]
    head_on = remote(wins.at[groups], head, hs.at[1], hr.at[1], {"seq": ahead})
    soft = HEAD_WIDTH ** (-0.5)

    def shifted(rows_a, by):
        pick = lax.broadcasted_iota(jnp.int32, (GROUP, 2 * GROUP), 1) == (
            lax.broadcasted_iota(jnp.int32, (GROUP, 2 * GROUP), 0) + by
        )
        return mm(jnp.where(pick, 1.0, 0.0).astype(BF16), rows_a).astype(BF16)

    def attend(g):
        table_e[g]["fwd_r"].wait_recv()
        table_e[g]["fwd_l"].wait_recv()
        enc = eb[g].reshape(keys, wide)
        kk = mm(enc, wk[...]).astype(BF16)
        vv = mm(enc, wv[...]).astype(BF16)
        if g == groups - 1:
            q_back.wait_recv()
            both = jnp.concatenate([q_ref[g * GROUP : (g + 1) * GROUP, :], qnext[...]], axis=0)
        else:
            both = q_ref[g * GROUP : (g + 2) * GROUP, :]
        qg = shifted(both, GROUP - 1)
        for h in range(heads):
            at = slice(h * HEAD_WIDTH, (h + 1) * HEAD_WIDTH)
            logits = lax.dot_general(qg[:, at], kk[:, at], NT, preferred_element_type=F32) * soft
            expo = jnp.exp(logits)
            probs = (expo * (1.0 / jnp.sum(expo, axis=-1, keepdims=True))).astype(BF16)
            wins[g + 1, :, at] = mm(probs, vv[:, at]).astype(BF16)

    order = [groups - 1] + list(range(groups - 1))

    def own_out(k):
        table_e[order[k]]["own_r"].start()
        table_e[order[k]]["own_l"].start()

    def onward(k):
        c = table_e[order[k]]
        c["own_r"].wait_recv()
        c["fwd_r"].start()
        c["own_l"].wait_recv()
        c["fwd_l"].start()

    own_out(0)
    own_out(1)
    loads[2].wait()
    loads[3].wait()
    onward(0)
    own_out(2)
    onward(1)
    own_out(3)
    attend(order[0])
    head_on.start()
    onward(2)
    attend(order[1])
    onward(3)
    attend(order[2])
    head_on.wait_recv()
    at_start = jnp.where(me == 0, 0.0, 1.0)
    wins[0] = jnp.where(at_start > 0.0, head[...].astype(F32), 0.0).astype(BF16)
    attend(order[3])

    def drain(k, c):
        peer = lax.rem(me + k, n)
        ids_copy(peer).wait_send()
        rows_copy(peer).wait_send()
        return c

    lax.fori_loop(1, n, drain, 0)
    for g in range(groups):
        for copy in table_e[g].values():
            copy.wait_send()
    for copy in in_r + in_l + on[0] + on[1] + twin_3[0] + twin_3[1] + twins[0] + twins[1] + x_r + x_l + x_on_r + x_on_l + [
        twin_12, lot_r, lot_l, lot_on_r, lot_on_l,
        hop_r, hop_l, give_r, give_l, far_r, far_l, q_back, head_on,
    ]:
        copy.wait_send()


def per_device(n, queries, vocab_rows, neighbour_ids, w_in, w_out, w_key, w_value):
    groups = neighbour_ids.shape[0]
    ids = neighbour_ids.reshape(1, -1)
    rows = ids.shape[1]
    cap = 2 * rows // n
    plane = PLANE
    feats = vocab_rows.shape[1]
    tok, width = queries.shape
    wide, hidden = w_in.shape
    keys = rows // groups
    part = keys // 4
    vm = lambda shape, dt=BF16: pltpu.VMEM(shape, dt)
    dma = pltpu.SemaphoreType.DMA
    windows = pl.pallas_call(
        functools.partial(layer_kernel, n, groups, plane, cap),
        out_shape=jax.ShapeDtypeStruct((groups + 1, GROUP, width), BF16),
        in_specs=[pl.BlockSpec(memory_space=pltpu.VMEM)] * 3 + [pl.BlockSpec(memory_space=pltpu.MemorySpace.HBM)] * 4,
        out_specs=pl.BlockSpec(memory_space=pltpu.VMEM),
        scratch_shapes=[
            vm((n, 1, 128), jnp.int32), vm((n, 1, 128), jnp.int32),
            vm((n, cap, feats)), vm((n, cap, feats)), vm((rows, feats), F32), vm((rows, 128), F32),
            vm((4, wide, hidden)), vm((4, hidden, wide)), vm(w_key.shape), vm(w_value.shape),
            vm((groups, 4, part, feats)),
            vm((groups, part // 2, feats)), vm((groups, part // 2, feats)),
            vm((4, groups, part, feats)), vm((4, keys, hidden)), vm((groups, 4, part, wide)),
            vm((GROUP, width)), vm((GROUP, width)),
            dma((4,)), dma((n,)), dma((n,)), dma((n,)), dma((n,)),
            dma((13,)), dma((13,)), dma((20,)), dma((20,)), dma((6,)), dma((6,)),
            dma((groups, 4)), dma((groups, 4)), dma((2,)), dma((2,)),
        ],
        compiler_params=pltpu.CompilerParams(
            collective_id=0, has_side_effects=True, vmem_limit_bytes=58 * 1024 * 1024
        ),
    )(ids, vocab_rows, queries, w_in, w_out, w_key, w_value)
    return windows.reshape((groups + 1) * GROUP, width)[1 : 1 + tok]


def solution(mesh):
    return jax.shard_map(
        functools.partial(per_device, mesh.shape["seq"]),
        mesh=mesh,
        in_specs=(
            P("seq", "tp"),
            P("seq", "tp"),
            P("seq", None, None),
            P(None, "tp"),
            P("tp", None),
            P(None, "tp"),
            P(None, "tp"),
        ),
        out_specs=P("seq", "tp"),
        check_vma=False,
    )
```

```python
import functools

import jax
import jax.numpy as jnp
from jax import lax
from jax.experimental import pallas as pl
from jax.experimental.pallas import tpu as pltpu
from jax.sharding import PartitionSpec as P

HEAD_WIDTH = 128
GROUP = 64
F32 = jnp.float32
BF16 = jnp.bfloat16
MESH = pl.DeviceIdType.MESH
PLANE = 8
NT = (((1,), (1,)), ((), ()))


def mm(a, b):
    return jnp.dot(a, b, preferred_element_type=F32)


def layer_kernel(n, groups, plane, cap, ids_ref, vocab_ref, q_ref, win_hbm, wout_hbm, wk_hbm, wv_hbm, wins,
                 want, req, sendb, recvb, acc, slots, win, wout, wk, wv, ob, relay_r, relay_l, xb, inner, eb,
                 qnext, head,
                 wsem, isend, irecv, rsend, rrecv, dsend, drecv, ssend, srecv, asend, arecv, es, er, hs, hr, spread):
    tp = 4
    t = lax.axis_index("tp")
    me = lax.axis_index("seq")
    right, left, across = lax.rem(t + 1, tp), lax.rem(t + tp - 1, tp), lax.rem(t + 2, tp)
    ahead, back = lax.rem(me + 1, n), lax.rem(me + n - 1, n)
    planes = n // plane
    mine = me // plane
    rows = ids_ref.shape[1]
    voc, feats = vocab_ref.shape
    block = plane * cap
    shift = voc.bit_length() - 1
    keys = rows // groups
    part = keys // 4
    wide = win.shape[1]
    hidden = win.shape[2]
    width = q_ref.shape[1]
    heads = width // HEAD_WIDTH

    base = (me // 8) * 8
    p = lax.rem(me, 8)
    core = lax.rem(me, 2)
    p_r, p_l, p_x = lax.rem(p + 2, 8), lax.rem(p + 6, 8), lax.rem(p + 4, 8)
    RIGHT, LEFT = {"tp": right}, {"tp": left}
    XR, XL, TWIN = {"seq": base + p_r}, {"seq": base + p_l}, {"seq": me + 1 - 2 * core}
    OTHER = 1 - core

    loads = [
        pltpu.make_async_copy(a, b, wsem.at[i])
        for i, (a, b) in enumerate([(win_hbm, win.at[0]), (wout_hbm, wout.at[0]), (wk_hbm, wk), (wv_hbm, wv)])
    ]
    for load in loads:
        load.start()

    barrier = pltpu.get_barrier_semaphore()

    def step_of(i):
        half = (i + 1) // 2
        return lax.rem(planes // 2 + jnp.where(lax.rem(i, 2) == 1, -half, half) + planes, planes)

    depth = n // 8
    up, down = {"seq": lax.rem(me + 8, n)}, {"seq": lax.rem(me + n - 8, n)}
    near = [RIGHT, LEFT, XR, XL, TWIN] + ([up, down] if depth > 2 else [])
    for where in near:
        pl.semaphore_signal(barrier, inc=1, device_id=where, device_id_type=MESH)

    pl.semaphore_wait(barrier, len(near))

    def remote(src, dst, ssem, rsem, where):
        return pltpu.make_async_remote_copy(
            src_ref=src, dst_ref=dst, send_sem=ssem, recv_sem=rsem, device_id=where, device_id_type=MESH
        )

    def ids_copy(peer):
        return remote(want.at[peer], req.at[me], isend.at[peer], irecv.at[me], {"seq": peer})

    def ids_arrival(src):
        return remote(want.at[src], req.at[src], isend.at[src], irecv.at[src], {"seq": src})

    def rows_copy(peer):
        return remote(sendb.at[peer], recvb.at[me], rsend.at[peer], rrecv.at[me], {"seq": peer})

    def rows_arrival(src):
        return remote(sendb.at[src], recvb.at[src], rsend.at[src], rrecv.at[src], {"seq": src})

    def send_ids(i, c):
        to = lax.rem(mine + step_of(i), planes)
        for j in range(plane):
            peer = to * plane + j

            @pl.when(peer != me)
            def _():
                ids_copy(peer).start()

        return c

    quarter = wide // 4

    def a_part(c, k):
        return pl.ds(pl.multiple_of(c * (2 * quarter) + k * quarter, quarter), quarter)

    def a_half(c):
        return pl.ds(pl.multiple_of(c * (2 * quarter), 2 * quarter), 2 * quarter)

    lot = hidden // 8
    lot2 = lot // 2

    def b_lot(i):
        return pl.ds(pl.multiple_of(i * lot, lot), lot)

    def b_half(i, k):
        return pl.ds(pl.multiple_of(i * lot + k * lot2, lot2), lot2)

    in_r = [remote(win_hbm.at[a_part(core, k)], win.at[1, a_part(core, k)], dsend.at[k], drecv.at[k], RIGHT) for k in (0, 1)]
    in_l = [remote(win_hbm.at[a_part(core, k)], win.at[2, a_part(core, k)], dsend.at[2 + k], drecv.at[2 + k], LEFT) for k in (0, 1)]
    eighth = quarter // 2

    def a_sub(c, k, j):
        return pl.ds(pl.multiple_of(c * (2 * quarter) + k * quarter + j * eighth, eighth), eighth)

    def a_on(k, j):
        at = a_sub(core, k, j)
        return remote(win.at[1 + k, at], win.at[3, at], dsend.at[4 + 2 * j + k], drecv.at[4 + 2 * j + k], (RIGHT, LEFT)[k])

    def a_twin(c, k, j):
        at = a_sub(c, k, j)
        return remote(win.at[3, at], win.at[3, at], dsend.at[8 + 2 * j + k], drecv.at[8 + 2 * j + k], TWIN)

    def a_twins(c):
        both = win.at[pl.ds(1, 2), a_half(c)]
        return remote(both, both, dsend.at[12], drecv.at[12], TWIN)

    on = [[a_on(k, j) for k in (0, 1)] for j in (0, 1)]
    twin_3 = [[a_twin(core, k, j) for k in (0, 1)] for j in (0, 1)]
    twin_12 = a_twins(core)
    lot_r = remote(wout_hbm.at[b_lot(p)], wout.at[1, b_lot(p)], ssend.at[0], srecv.at[0], RIGHT)
    lot_l = remote(wout_hbm.at[b_lot(p)], wout.at[2, b_lot(p)], ssend.at[1], srecv.at[1], LEFT)
    lot_on_r = remote(wout.at[1, b_half(p, 0)], wout.at[3, b_half(p, 0)], ssend.at[2], srecv.at[2], RIGHT)
    lot_on_l = remote(wout.at[2, b_half(p, 1)], wout.at[3, b_half(p, 1)], ssend.at[3], srecv.at[3], LEFT)
    slots_of = (pl.ds(1, 2), pl.ds(3, 1))

    def share(m, at, i, where):
        both = wout.at[slots_of[m], at]
        return remote(both, both, ssend.at[4 + 8 * m + i], srecv.at[4 + 8 * m + i], where)

    x_r = [share(m, b_lot(p), 0, XR) for m in (0, 1)]
    x_l = [share(m, b_lot(p), 1, XL) for m in (0, 1)]
    x_on_r = [share(m, b_half(p_l, 0), 2, XR) for m in (0, 1)]
    x_on_l = [share(m, b_half(p_r, 1), 3, XL) for m in (0, 1)]
    twins = [[share(m, b_lot(q), 4 + i, TWIN) for i, q in enumerate((p, p_l, p_r, p_x))] for m in (0, 1)]

    def x_start(m):
        x_r[m].start()
        x_l[m].start()
        twins[m][0].start()

    def x_forward(m):
        x_r[m].wait_recv()
        x_l[m].wait_recv()
        x_on_r[m].start()
        x_on_l[m].start()
        twins[m][1].start()
        twins[m][2].start()

    def x_finish(m):
        x_on_r[m].wait_recv()
        x_on_l[m].wait_recv()
        twins[m][3].start()

    lot_r.start()
    lot_l.start()
    in_r[0].start()
    in_l[1].start()
    q_back = remote(q_ref.at[pl.ds(0, GROUP)], qnext, hs.at[0], hr.at[0], {"seq": back})
    def tell(i, where):
        pl.semaphore_signal(spread.at[i], inc=1, device_id=where, device_id_type=MESH)

    def heard(i):
        pl.semaphore_wait(spread.at[i], 1)

    tell(0, TWIN)
    ids = ids_ref[...]
    owner = ids >> shift
    local = ids & (voc - 1)
    hot = jnp.where(lax.broadcasted_iota(jnp.int32, (n, rows), 0) == owner, 1.0, 0.0).astype(F32)
    hot16 = hot.astype(BF16)
    before = jnp.where(
        lax.broadcasted_iota(jnp.int32, (rows, rows), 0) < lax.broadcasted_iota(jnp.int32, (rows, rows), 1), 1.0, 0.0
    ).astype(BF16)
    count = mm(hot16, before)
    rank = jnp.sum(hot * count, axis=0, keepdims=True).astype(jnp.int32)
    heard(0)
    tell(1, XR)
    tell(2, XL)
    ranked = lax.broadcasted_iota(jnp.int32, (128, rows), 0) == rank
    low = jnp.where(ranked, (local & 255).astype(F32), 0.0).astype(BF16)
    high = jnp.where(ranked, (local >> 8).astype(F32), 0.0).astype(BF16)
    table = lax.dot_general(hot16, low, NT, preferred_element_type=F32) + 256.0 * lax.dot_general(
        hot16, high, NT, preferred_element_type=F32
    )
    heard(1)
    heard(2)
    tell(3, XR)
    table = table.astype(jnp.int32)
    for o in range(n):
        want[o] = table[o : o + 1]

    heard(3)
    for step in range(depth // 2):
        tell(4 + 2 * step, up)
        tell(5 + 2 * step, down)
        if step == 0:
            slot = (owner * cap + rank).astype(F32)
            slots[...] = jnp.transpose(jnp.broadcast_to(slot, (128, rows)))
        heard(4 + 2 * step)
        heard(5 + 2 * step)
    if depth < 2:
        slot = (owner * cap + rank).astype(F32)
        slots[...] = jnp.transpose(jnp.broadcast_to(slot, (128, rows)))

    lax.fori_loop(0, planes, send_ids, 0)
    q_back.start()
    req[me] = want[me]


    def answer(i, c):
        to = lax.rem(mine + step_of(i), planes)
        for j in range(plane):
            peer = to * plane + j

            @pl.when(peer != me)
            def _():
                ids_arrival(peer).wait_recv()

        @pl.when(i == 0)
        def _():
            lot_r.wait_recv()
            lot_on_r.start()
            lot_l.wait_recv()
            lot_on_l.start()
            x_start(0)
            in_r[1].start()
            in_l[0].start()

        asked = jnp.concatenate([req[to * plane + j] for j in range(plane)], axis=0).astype(F32)
        asked = jnp.transpose(jnp.concatenate([asked, jnp.zeros((128 - plane, 128), F32)], axis=0))
        cols = [jnp.broadcast_to(asked[:cap, j : j + 1], (cap, 128)) for j in range(plane)]
        col = jnp.concatenate(cols, axis=0)
        total = jnp.zeros((block, feats), F32)
        deep = min(256, voc)
        for v in range(0, voc, deep):
            picks = [
                jnp.where(
                    col == (lax.broadcasted_iota(jnp.int32, (block, 128), 1) + (v + w)).astype(F32), 1.0, 0.0
                ).astype(BF16)
                for w in range(0, deep, 128)
            ]
            total += mm(jnp.concatenate(picks, axis=1), vocab_ref[v : v + deep, :])
        found = total.astype(BF16)
        for j in range(plane):
            sendb[to * plane + j] = found[j * cap : (j + 1) * cap]
        for j in range(plane):
            peer = to * plane + j

            @pl.when(peer != me)
            def _():
                rows_copy(peer).start()

        return c

    lax.fori_loop(0, planes, answer, 0)
    recvb[me] = sendb[me]

    acc[...] = jnp.zeros_like(acc)

    def gather(i, c):
        @pl.when(i == 0)
        def _():
            in_r[0].wait_recv()
            on[0][0].start()
            on[1][0].start()
            in_l[1].wait_recv()
            on[0][1].start()
            on[1][1].start()

        @pl.when(i == 1)
        def _():
            lot_on_r.wait_recv()
            lot_on_l.wait_recv()
            x_start(1)

        @pl.when(i == 3)
        def _():
            x_forward(0)

        @pl.when(i == 5)
        def _():
            in_r[1].wait_recv()
            in_l[0].wait_recv()
            twin_12.start()

        source = lax.rem(mine - step_of(i) + planes, planes)
        for j in range(plane):
            src = source * plane + j

            @pl.when(src != me)
            def _():
                rows_arrival(src).wait_recv()

        first = (source * block).astype(F32)
        at = slots[...] - first
        picks = [
            jnp.where(at == (lax.broadcasted_iota(jnp.int32, (rows, 128), 1) + w).astype(F32), 1.0, 0.0).astype(BF16)
            for w in range(0, block, 128)
        ]
        got = jnp.concatenate([recvb[source * plane + j] for j in range(plane)], axis=0)
        acc[...] += mm(jnp.concatenate(picks, axis=1), got)
        return c

    lax.fori_loop(0, planes, gather, 0)

    ob[...] = acc[...].reshape(groups, 4, part, feats).astype(BF16)
    low_part, high_part = pl.ds(0, part // 2), pl.ds(part // 2, part // 2)
    hop_r = remote(ob.at[:, across, low_part], relay_r, asend.at[0], arecv.at[0], RIGHT)
    hop_l = remote(ob.at[:, across, high_part], relay_l, asend.at[1], arecv.at[1], LEFT)
    give_r = remote(ob.at[:, right], xb.at[1], asend.at[2], arecv.at[2], RIGHT)
    give_l = remote(ob.at[:, left], xb.at[2], asend.at[3], arecv.at[3], LEFT)
    far_r = remote(relay_r, xb.at[3, :, low_part], asend.at[4], arecv.at[4], RIGHT)
    far_l = remote(relay_l, xb.at[3, :, high_part], asend.at[5], arecv.at[5], LEFT)
    hop_r.start()
    hop_l.start()
    give_r.start()
    give_l.start()
    xb[0] = ob[:, t]
    x_forward(1)
    hop_r.wait_recv()
    far_r.start()
    hop_l.wait_recv()
    far_l.start()
    for j in (0, 1):
        for k in (0, 1):
            on[j][k].wait_recv()
            twin_3[j][k].start()
    x_finish(0)
    for copy in (give_r, give_l, far_r, far_l):
        copy.wait_recv()

    slices = [t, left, right, across]

    def feature(i):
        return pl.ds(pl.multiple_of(slices[i] * feats, feats), feats)

    square = jnp.zeros((keys, 1), F32)
    for i in range(4):
        v = xb[i].reshape(keys, feats).astype(F32)
        square += jnp.sum(v * v, axis=-1, keepdims=True)
    scale = lax.rsqrt(square * (1.0 / wide) + 1e-06)
    normed = [(xb[i].reshape(keys, feats).astype(F32) * scale).astype(BF16) for i in range(4)]

    def twin_arrival(i):
        if i == 1:
            a_twins(OTHER).wait_recv()
        if i == 3:
            for j in (0, 1):
                for k in (0, 1):
                    a_twin(OTHER, k, j).wait_recv()

    loads[0].wait()
    for i in range(4):
        if i == 2:
            x_finish(1)
        twin_arrival(i)
        hid = jnp.zeros((keys, hidden), F32)
        for f in range(4):
            hid += mm(normed[f], win[i, feature(f), :])
        inner[i] = jax.nn.gelu(hid, approximate=True).astype(BF16)
    loads[1].wait()
    for i, q in enumerate((p, p_l, p_r, p_x)):
        for m in (0, 1):
            share(m, b_lot(q + 1 - 2 * core), 4 + i, TWIN).wait_recv()
    for f in range(4):
        total = xb[f].reshape(keys, feats).astype(F32)
        for i in range(4):
            total += mm(inner[i], wout[i, :, feature(f)])
        total = total.astype(BF16)
        for g in range(groups):
            eb[g, 0, :, feature(f)] = total[g * part : (g + 1) * part]

    def ring(g):
        own = eb.at[g, 0]
        return dict(
            own_r=remote(own, eb.at[g, 1], es.at[g, 0], er.at[g, 0], RIGHT),
            own_l=remote(own, eb.at[g, 2], es.at[g, 1], er.at[g, 1], LEFT),
            fwd_r=remote(eb.at[g, 1, low_part], eb.at[g, 3, low_part], es.at[g, 2], er.at[g, 2], RIGHT),
            fwd_l=remote(eb.at[g, 2, high_part], eb.at[g, 3, high_part], es.at[g, 3], er.at[g, 3], LEFT),
        )

    table_e = [ring(g) for g in range(groups)]
    head_on = remote(wins.at[groups], head, hs.at[1], hr.at[1], {"seq": ahead})
    soft = HEAD_WIDTH ** (-0.5)

    def shifted(rows_a, by):
        pick = lax.broadcasted_iota(jnp.int32, (GROUP, 2 * GROUP), 1) == (
            lax.broadcasted_iota(jnp.int32, (GROUP, 2 * GROUP), 0) + by
        )
        return mm(jnp.where(pick, 1.0, 0.0).astype(BF16), rows_a).astype(BF16)

    def attend(g):
        table_e[g]["fwd_r"].wait_recv()
        table_e[g]["fwd_l"].wait_recv()
        enc = eb[g].reshape(keys, wide)
        kk = mm(enc, wk[...]).astype(BF16)
        vv = mm(enc, wv[...]).astype(BF16)
        if g == groups - 1:
            q_back.wait_recv()
            both = jnp.concatenate([q_ref[g * GROUP : (g + 1) * GROUP, :], qnext[...]], axis=0)
        else:
            both = q_ref[g * GROUP : (g + 2) * GROUP, :]
        qg = shifted(both, GROUP - 1)
        for h in range(heads):
            at = slice(h * HEAD_WIDTH, (h + 1) * HEAD_WIDTH)
            logits = lax.dot_general(qg[:, at], kk[:, at], NT, preferred_element_type=F32) * soft
            expo = jnp.exp(logits)
            probs = (expo * (1.0 / jnp.sum(expo, axis=-1, keepdims=True))).astype(BF16)
            wins[g + 1, :, at] = mm(probs, vv[:, at]).astype(BF16)

    order = [groups - 1] + list(range(groups - 1))

    def own_out(k):
        table_e[order[k]]["own_r"].start()
        table_e[order[k]]["own_l"].start()

    def onward(k):
        c = table_e[order[k]]
        c["own_r"].wait_recv()
        c["fwd_r"].start()
        c["own_l"].wait_recv()
        c["fwd_l"].start()

    own_out(0)
    own_out(1)
    loads[2].wait()
    loads[3].wait()
    onward(0)
    own_out(2)
    onward(1)
    own_out(3)
    attend(order[0])
    head_on.start()
    onward(2)
    attend(order[1])
    onward(3)
    attend(order[2])
    head_on.wait_recv()
    at_start = jnp.where(me == 0, 0.0, 1.0)
    wins[0] = jnp.where(at_start > 0.0, head[...].astype(F32), 0.0).astype(BF16)
    attend(order[3])

    def drain(k, c):
        peer = lax.rem(me + k, n)
        ids_copy(peer).wait_send()
        rows_copy(peer).wait_send()
        return c

    lax.fori_loop(1, n, drain, 0)
    for g in range(groups):
        for copy in table_e[g].values():
            copy.wait_send()
    for copy in in_r + in_l + on[0] + on[1] + twin_3[0] + twin_3[1] + twins[0] + twins[1] + x_r + x_l + x_on_r + x_on_l + [
        twin_12, lot_r, lot_l, lot_on_r, lot_on_l,
        hop_r, hop_l, give_r, give_l, far_r, far_l, q_back, head_on,
    ]:
        copy.wait_send()


def per_device(n, queries, vocab_rows, neighbour_ids, w_in, w_out, w_key, w_value):
    groups = neighbour_ids.shape[0]
    ids = neighbour_ids.reshape(1, -1)
    rows = ids.shape[1]
    cap = 2 * rows // n
    plane = PLANE
    feats = vocab_rows.shape[1]
    tok, width = queries.shape
    wide, hidden = w_in.shape
    keys = rows // groups
    part = keys // 4
    vm = lambda shape, dt=BF16: pltpu.VMEM(shape, dt)
    dma = pltpu.SemaphoreType.DMA
    windows = pl.pallas_call(
        functools.partial(layer_kernel, n, groups, plane, cap),
        out_shape=jax.ShapeDtypeStruct((groups + 1, GROUP, width), BF16),
        in_specs=[pl.BlockSpec(memory_space=pltpu.VMEM)] * 3 + [pl.BlockSpec(memory_space=pltpu.MemorySpace.HBM)] * 4,
        out_specs=pl.BlockSpec(memory_space=pltpu.VMEM),
        scratch_shapes=[
            vm((n, 1, 128), jnp.int32), vm((n, 1, 128), jnp.int32),
            vm((n, cap, feats)), vm((n, cap, feats)), vm((rows, feats), F32), vm((rows, 128), F32),
            vm((4, wide, hidden)), vm((4, hidden, wide)), vm(w_key.shape), vm(w_value.shape),
            vm((groups, 4, part, feats)),
            vm((groups, part // 2, feats)), vm((groups, part // 2, feats)),
            vm((4, groups, part, feats)), vm((4, keys, hidden)), vm((groups, 4, part, wide)),
            vm((GROUP, width)), vm((GROUP, width)),
            dma((4,)), dma((n,)), dma((n,)), dma((n,)), dma((n,)),
            dma((13,)), dma((13,)), dma((20,)), dma((20,)), dma((6,)), dma((6,)),
            dma((groups, 4)), dma((groups, 4)), dma((2,)), dma((2,)), pltpu.SemaphoreType.REGULAR((12,)),
        ],
        compiler_params=pltpu.CompilerParams(
            collective_id=0, has_side_effects=True, vmem_limit_bytes=58 * 1024 * 1024
        ),
    )(ids, vocab_rows, queries, w_in, w_out, w_key, w_value)
    return windows.reshape((groups + 1) * GROUP, width)[1 : 1 + tok]


def solution(mesh):
    return jax.shard_map(
        functools.partial(per_device, mesh.shape["seq"]),
        mesh=mesh,
        in_specs=(
            P("seq", "tp"),
            P("seq", "tp"),
            P("seq", None, None),
            P(None, "tp"),
            P("tp", None),
            P(None, "tp"),
            P(None, "tp"),
        ),
        out_specs=P("seq", "tp"),
        check_vma=False,
    )
```
